32 devices in a mesh: row: 4 (over x, core), col: 8 (over z, y).
Axes of the slice: x: 2, y: 2, z: 4, core: 2. Of those that a mesh axis runs over, the one named last changes fastest.
Arguments:
- vectors: bfloat16 [32, 8192], P(None, ('row', 'col')), may hold values from -6 to 6
- tiles: bfloat16 [512, 256, 256], P(('row', 'col')), may hold values from -0.09375 to 0.09375
- tile_rows: int32 [512], P(('row', 'col')), may hold values from 0 to 7, as said below
- tile_cols: int32 [512], P(('row', 'col')), may hold values from 0 to 3, as said below
- tile_live: int32 [32], P(('row', 'col')), may hold values from 2 to 16, as said below
Outputs:
- first: bfloat16 [32, 8192], P(None, ('row', 'col'))
- second: bfloat16 [32, 8192], P(None, ('row', 'col'))
The draws below stay inside these ranges and needn't reach their ends.
Inputs may be any that keep to these rules, and one draw needn't show every extreme that they name: `tile_rows`: A slot's row block is counted among the 8 row blocks of its device's row index, and its global row block never exceeds its global column block. `tile_cols`: A slot's column block is counted among the 4 column blocks of its device's column index. Each device uses its first tile_live slots; some device uses all 16.
All inputs are finite; a program needn't handle non-finite values.
Results may differ from the reference program's by a relative error of at most 0.0044.
Values may be sent and summed in bfloat16 or wider, within the bound.
No kernel may reach another device: no remote copies, remote signals or barrier semaphores. Data moves between devices by JAX's collectives and lax.ppermute only.
A program may use at most 64 MiB of HBM per device.

```python
import jax
import jax.numpy as jnp
from jax import lax

BS = 256
K = 32
VB = 1
TILES = 16
ROWSET = 8
COLSET = 4
ORDER = 8192
DEVICES = 32


def tile_layout(key):
    ncol = ROWSET // VB
    nrow = COLSET // VB
    slot = jnp.arange(DEVICES * TILES, dtype=jnp.int32)
    device = slot // TILES
    rowidx = device // ncol
    colidx = device % ncol
    base = jax.random.fold_in(key, 7)
    key_p = jax.random.fold_in(base, 1)
    key_e = jax.random.fold_in(base, 2)
    key_a = jax.random.fold_in(base, 3)
    part_p = rowidx + jax.random.randint(key_p, slot.shape, 0, nrow - rowidx)
    part_e = jax.random.randint(key_e, slot.shape, 0, VB)
    upper = jnp.where(part_p == rowidx, colidx * VB + part_e, ROWSET - 1)
    local_a = jax.random.randint(key_a, slot.shape, 0, upper + 1)
    return (local_a.astype(jnp.int32), (part_p * VB + part_e).astype(jnp.int32))


def draw_tile_rows(key, part):
    return tile_layout(key)[0]


def draw_tile_cols(key, part):
    return tile_layout(key)[1]


def draw_tile_live(key, part):
    key_s = jax.random.fold_in(key, 11)
    key_i = jax.random.fold_in(key, 12)
    key_j = jax.random.fold_in(key, 13)
    shifts = jax.random.randint(key_s, (DEVICES,), 0, 4)
    live = jnp.right_shift(jnp.full((DEVICES,), TILES, jnp.int32), shifts)
    first_dev = jax.random.randint(key_i, (), 0, DEVICES)
    other_dev = (first_dev + 1 + jax.random.randint(key_j, (), 0, DEVICES - 1)) % DEVICES
    live = live.at[first_dev].set(TILES)
    live = live.at[other_dev].set(TILES // 8)
    return live.astype(jnp.int32)


def levels(stream_key, dims, pieces, low, high):
    factor_of = 1.0
    for position, blocks in pieces:
        steps = jax.random.uniform(jax.random.fold_in(jax.random.fold_in(stream_key, 6), position), (blocks,), jnp.float32, low / len(pieces), high / len(pieces))
        factor_of = factor_of * jnp.repeat(jnp.exp(steps), dims[position] // blocks).reshape((-1,) + (1,) * (len(dims) - 1 - position))
    return factor_of


def noise(stream_key, extent, width, bound, split=(), kind=jnp.bfloat16):
    array = width * jax.random.normal(stream_key, extent, jnp.float32)
    if split:
        array = array * levels(stream_key, extent, split, -0.22, 0.18)
    return jnp.clip(array, -bound, bound).astype(kind)


def setup_inputs(seed: int = 0) -> dict:
    arg_keys = jax.random.split(jax.random.key(seed), 6)
    return {
        "vectors": noise(arg_keys[0], (K, ORDER), 1.0, 6.0, ((1, 32),)),
        "tiles": noise(arg_keys[1], (DEVICES * TILES, BS, BS), (BS * TILES) ** -0.5, 0.09375, ((0, 32),)),
        "tile_rows": draw_tile_rows(jax.random.fold_in(arg_keys[5], 71), 0),
        "tile_cols": draw_tile_cols(jax.random.fold_in(arg_keys[5], 71), 0),
        "tile_live": draw_tile_live(jax.random.fold_in(arg_keys[5], 71), 0),
    }


def reference(vectors, tiles, tile_rows, tile_cols, tile_live):
    ncol = ROWSET // VB
    nblocks = DEVICES * VB
    slot = jnp.arange(DEVICES * TILES, dtype=jnp.int32)
    device = slot // TILES
    rowidx = device // ncol
    colidx = device % ncol
    grow = (rowidx * ROWSET + tile_rows).astype(jnp.int32)
    part_p = tile_cols // VB
    part_e = tile_cols % VB
    gcol = ((part_p * ncol + colidx) * VB + part_e).astype(jnp.int32)
    keep = ((slot % TILES) < tile_live[device]).astype(jnp.float32)

    def apply(vec):
        blocks = vec.reshape(K, nblocks, BS)

        def step(acc, group):
            tile_g, row_g, col_g, keep_g = group
            tile_f = tile_g.astype(jnp.float32)
            pick_c = blocks[:, col_g].astype(jnp.float32)
            pick_r = blocks[:, row_g].astype(jnp.float32)
            direct = jnp.einsum("ktj,tij->kti", pick_c, tile_f) * keep_g[None, :, None]
            mirror = jnp.einsum("kti,tij->ktj", pick_r, tile_f) * keep_g[None, :, None]
            acc = acc.at[:, row_g].add(direct)
            acc = acc.at[:, col_g].add(mirror)
            return acc, None

        groups = (tiles.reshape(DEVICES, TILES, BS, BS), grow.reshape(DEVICES, TILES),
                  gcol.reshape(DEVICES, TILES), keep.reshape(DEVICES, TILES))
        init = jnp.zeros((K, nblocks, BS), jnp.float32)
        total, _ = lax.scan(step, init, groups)
        return total.reshape(K, nblocks * BS)

    first_f = apply(vectors)
    first = first_f.astype(jnp.bfloat16)
    second = (2.0 * apply(first) - vectors.astype(jnp.float32)).astype(jnp.bfloat16)
    return first, second
```

```python
import functools

import jax
import jax.numpy as jnp
from jax import lax
from jax.experimental import pallas as pl
from jax.experimental.pallas import tpu as pltpu
from jax.sharding import PartitionSpec as P


def digits_of(count):
    out, stride, rest, prime = [], 1, count, 2
    while rest > 1:
        while rest % prime:
            prime += 1
        out.append((stride, prime))
        stride, rest = stride * prime, rest // prime
    return out


def moved(index, stride, radix, step):
    digit = index // stride % radix
    return index + ((digit + step) % radix - digit) * stride


def send(value, axis, count, stride, radix, step):
    pairs = [(i, moved(i, stride, radix, step)) for i in range(count)]
    return lax.ppermute(value, axis, pairs)


def gather(block, axis, count):
    pieces = [block[None]]
    for stride, radix in reversed(digits_of(count)):
        held = pieces[0] if len(pieces) == 1 else jnp.concatenate(pieces, 0)
        for step in range(1, radix):
            pieces.append(send(held, axis, count, stride, radix, -step))
    return pieces


def slots_of(count):
    slots = [()]
    for _, radix in reversed(digits_of(count)):
        slots = [(step,) + rest for step in range(radix) for rest in slots]
    return slots


def slot_index(me, count, steps):
    for (stride, radix), step in zip(digits_of(count), steps):
        if step:
            me = moved(me, stride, radix, step)
    return me


def sizes_of(count):
    sizes, held = [1], 1
    for _, radix in reversed(digits_of(count)):
        sizes += [held] * (radix - 1)
        held *= radix
    return sizes


def scatter(pieces, axis, count):
    for stride, radix in digits_of(count):
        keep = pieces[: len(pieces) - (radix - 1)]
        sent = pieces[len(keep) :]
        got = [send(value, axis, count, stride, radix, step + 1) for step, value in enumerate(sent)]
        at, pieces = 0, []
        for value in keep:
            size = value.shape[0]
            for other in got:
                value = value + other[at : at + size]
            at += size
            pieces.append(value)
    return pieces[0][0]


def kernel(me_ref, take_ref, put_ref, live_ref, *refs, n_in, counts, axes, direct):
    pieces, tiles_ref, outs = refs[:n_in], refs[n_in], refs[n_in + 1 : -2]
    vec, acc = refs[-2:]
    count_in, count_out = counts
    me_in, me_out = me_ref[0], me_ref[1]
    slots = iter(slots_of(count_in))
    for piece in pieces:
        for i in range(piece.shape[0]):
            vec[slot_index(me_in, count_in, next(slots))] = piece[i]
    acc[...] = jnp.zeros_like(acc)
    dims = (((1,), (1,)), ((), ())) if direct else (((1,), (0,)), ((), ()))
    live = live_ref[0]
    for t in range(tiles_ref.shape[0]):
        x = vec[take_ref[t]]
        y = lax.dot_general(x, tiles_ref[t], dims, preferred_element_type=jnp.float32)
        acc[put_ref[t]] += jnp.where(t < live, y, 0.0)
    slots = iter(slots_of(count_out))
    for out in outs:
        for i in range(out.shape[0]):
            out[i] = acc[slot_index(me_out, count_out, next(slots))]


def half(me, pieces, tiles, take, put, live, counts, direct):
    width, size = pieces[0].shape[1:]
    smem = pl.BlockSpec(memory_space=pltpu.SMEM)
    vmem = pl.BlockSpec(memory_space=pltpu.VMEM)
    sizes = sizes_of(counts[1])
    return pl.pallas_call(
        functools.partial(kernel, n_in=len(pieces), counts=counts, axes=None, direct=direct),
        out_shape=[jax.ShapeDtypeStruct((n, width, size), jnp.float32) for n in sizes],
        in_specs=[smem] * 4 + [vmem] * (len(pieces) + 1),
        out_specs=[vmem] * len(sizes),
        scratch_shapes=[
            pltpu.VMEM((counts[0], width, size), jnp.bfloat16),
            pltpu.VMEM((counts[1], width, size), jnp.float32),
        ],
        name="direct" if direct else "mirror",
    )(me, take, put, live, *pieces, tiles)


def local(rows, cols, vectors, tiles, tile_rows, tile_cols, tile_live):
    r, c = lax.axis_index("row"), lax.axis_index("col")
    me_direct = jnp.stack([r, c]).astype(jnp.int32)
    me_mirror = jnp.stack([c, r]).astype(jnp.int32)

    def apply(vec):
        colset = gather(vec, "row", rows)
        rowset = gather(vec, "col", cols)
        direct = half(me_direct, colset, tiles, tile_cols, tile_rows, tile_live, (rows, cols), True)
        mirror = half(me_mirror, rowset, tiles, tile_rows, tile_cols, tile_live, (cols, rows), False)
        return scatter(list(direct), "col", cols) + scatter(list(mirror), "row", rows)

    first = apply(vectors).astype(jnp.bfloat16)
    second = 2.0 * apply(first) - vectors.astype(jnp.float32)
    return first, second.astype(jnp.bfloat16)


def solution(mesh):
    both = ("row", "col")
    placed = (P(None, both), P(both, None, None), P(both), P(both), P(both))
    return jax.shard_map(
        functools.partial(local, mesh.shape["row"], mesh.shape["col"]),
        mesh=mesh,
        in_specs=placed,
        out_specs=(P(None, both), P(None, both)),
        check_vma=False,
    )
```

```python
import functools

import jax
import jax.numpy as jnp
from jax import lax
from jax.experimental import pallas as pl
from jax.experimental.pallas import tpu as pltpu
from jax.sharding import PartitionSpec as P

SMEM = pl.BlockSpec(memory_space=pltpu.SMEM)
VMEM = pl.BlockSpec(memory_space=pltpu.VMEM)
HBM = pl.BlockSpec(memory_space=pltpu.HBM)


def digits_of(count, wide):
    out, stride, rest = [], 1, count
    for radix in wide:
        if rest % radix == 0:
            out.append((stride, radix))
            stride, rest = stride * radix, rest // radix
    prime = 2
    while rest > 1:
        while rest % prime:
            prime += 1
        out.append((stride, prime))
        stride, rest = stride * prime, rest // prime
    return out


def moved(index, stride, radix, step):
    if radix & (radix - 1) == 0 and stride & (stride - 1) == 0:
        return index ^ (abs(step) * stride)
    digit = index // stride % radix
    return index + ((digit + step) % radix - digit) * stride


def send(value, axis, count, stride, radix, step):
    pairs = [(i, moved(i, stride, radix, step)) for i in range(count)]
    return lax.ppermute(value, axis, pairs)


def gather(block, kept, axis, count, digits):
    pieces = [kept[None]]
    for stride, radix in reversed(digits):
        held = block[None] if len(pieces) == 1 else jnp.concatenate(pieces, 0)
        for step in range(1, radix):
            pieces.append(send(held, axis, count, stride, radix, -step))
    return pieces


def slots_of(digits):
    slots = [()]
    for _, radix in reversed(digits):
        slots = [(step,) + rest for step in range(radix) for rest in slots]
    return slots


def slot_index(me, digits, steps):
    for (stride, radix), step in zip(digits, steps):
        if step:
            me = moved(me, stride, radix, step)
    return me


def sizes_of(digits):
    sizes, held = [1], 1
    for _, radix in reversed(digits):
        sizes += [held] * (radix - 1)
        held *= radix
    return sizes


def scatter(pieces, axis, count, digits):
    for stride, radix in digits:
        keep = pieces[: len(pieces) - (radix - 1)]
        sent = pieces[len(keep) :]
        got = [send(value, axis, count, stride, radix, step + 1) for step, value in enumerate(sent)]
        at, pieces = 0, []
        for value in keep:
            size = value.shape[0]
            for other in got:
                value = value + other[at : at + size]
            at += size
            pieces.append(value)
    return pieces[0][0]


def fetch_kernel(tiles_hbm, vec_hbm, tiles_ref, vec_ref, sems):
    pairs = ((tiles_hbm, tiles_ref), (vec_hbm, vec_ref))
    copies = [pltpu.make_async_copy(a, b, sems.at[i]) for i, (a, b) in enumerate(pairs)]
    for copy in copies:
        copy.start()
    for copy in copies:
        copy.wait()


def fetch(*arrays):
    return pl.pallas_call(
        fetch_kernel,
        out_shape=[jax.ShapeDtypeStruct(a.shape, a.dtype) for a in arrays],
        in_specs=[HBM] * 2,
        out_specs=[VMEM] * 2,
        scratch_shapes=[pltpu.SemaphoreType.DMA((2,))],
        compiler_params=pltpu.CompilerParams(vmem_limit_bytes=16 * 2**20),
        cost_estimate=pl.CostEstimate(flops=0, bytes_accessed=8 * 2**20, transcendentals=0),
        name="fetch",
    )(*[pltpu.with_memory_space_constraint(a, pltpu.HBM) for a in arrays])


def kernel(index_ref, *refs, n_in, plans, direct):
    pieces, tiles_ref, outs = refs[:n_in], refs[n_in], refs[n_in + 1 : -2]
    vec, acc = refs[-2:]
    slots = tiles_ref.shape[0]
    me_r, me_c = lax.axis_index("row"), lax.axis_index("col")
    me_in, me_out = (me_r, me_c) if direct else (me_c, me_r)
    where = iter(slots_of(plans[0]))
    for piece in pieces:
        for i in range(piece.shape[0]):
            vec[slot_index(me_in, plans[0], next(where))] = piece[i]
    acc[...] = jnp.zeros_like(acc)
    dims = (((1,), (1,)), ((), ())) if direct else (((1,), (0,)), ((), ()))
    live = index_ref[2 * slots]
    for t in range(slots):
        row, col = index_ref[t], index_ref[slots + t]
        take, put = (col, row) if direct else (row, col)
        y = lax.dot_general(vec[take], tiles_ref[t], dims, preferred_element_type=jnp.float32)
        acc[put] += jnp.where(t < live, y, 0.0)
    where = iter(slots_of(plans[1]))
    for out in outs:
        for i in range(out.shape[0]):
            out[i] = acc[slot_index(me_out, plans[1], next(where))]


def half(index, pieces, tiles, plans, direct):
    width, size = pieces[0].shape[1:]
    sizes = sizes_of(plans[1])
    count_in, count_out = (sum(sizes_of(plan)) for plan in plans)
    flops = 2 * width * tiles.size
    return pl.pallas_call(
        functools.partial(kernel, n_in=len(pieces), plans=plans, direct=direct),
        out_shape=[jax.ShapeDtypeStruct((n, width, size), jnp.float32) for n in sizes],
        in_specs=[SMEM] + [VMEM] * (len(pieces) + 1),
        out_specs=[VMEM] * len(sizes),
        scratch_shapes=[
            pltpu.VMEM((count_in, width, size), jnp.bfloat16),
            pltpu.VMEM((count_out, width, size), jnp.float32),
        ],
        compiler_params=pltpu.CompilerParams(vmem_limit_bytes=16 * 2**20),
        name="direct" if direct else "mirror",
    )(index, *pieces, tiles)


def local(rows, cols, vectors, tiles, tile_rows, tile_cols, tile_live):
    row_plan, col_plan = digits_of(rows, (4,)), digits_of(cols, ())
    index = jnp.concatenate([tile_rows, tile_cols, tile_live])
    held, vectors_held = fetch(tiles, vectors)

    def apply(vec, kept):
        colset = gather(vec, kept, "row", rows, row_plan)
        rowset = gather(vec, kept, "col", cols, col_plan)
        direct = half(index, colset, held, (row_plan, col_plan), True)
        mirror = half(index, rowset, held, (col_plan, row_plan), False)
        return scatter(list(direct), "col", cols, col_plan) + scatter(list(mirror), "row", rows, row_plan)

    first = apply(vectors, vectors_held).astype(jnp.bfloat16)
    second = 2.0 * apply(first, first) - vectors_held.astype(jnp.float32)
    return first, second.astype(jnp.bfloat16)


def solution(mesh):
    both = ("row", "col")
    placed = (P(None, both), P(both, None, None), P(both), P(both), P(both))
    return jax.shard_map(
        functools.partial(local, mesh.shape["row"], mesh.shape["col"]),
        mesh=mesh,
        in_specs=placed,
        out_specs=(P(None, both), P(None, both)),
        check_vma=False,
    )
```

```python
import functools
import math

import jax
import jax.numpy as jnp
from jax import lax
from jax.experimental import pallas as pl
from jax.experimental.pallas import tpu as pltpu
from jax.sharding import PartitionSpec as P

SMEM = pl.BlockSpec(memory_space=pltpu.SMEM)
VMEM = pl.BlockSpec(memory_space=pltpu.VMEM)
HBM = pl.BlockSpec(memory_space=pltpu.HBM)
PARAMS = pltpu.CompilerParams(vmem_limit_bytes=16 * 2**20)


def digits_of(count, wide):
    out, stride, rest, prime = [], 1, count, 2
    while rest > 1:
        while rest % prime:
            prime += 1
        radix = 4 if wide > 0 and rest % 4 == 0 else prime
        wide -= 1
        out.append((stride, radix))
        stride, rest = stride * radix, rest // radix
    return out


def moved(index, stride, radix, step):
    if radix & (radix - 1) == 0 and stride & (stride - 1) == 0:
        return index ^ (abs(step) * stride)
    digit = index // stride % radix
    return index + ((digit + step) % radix - digit) * stride


def send(value, axis, count, stride, radix, step):
    pairs = [(i, moved(i, stride, radix, step)) for i in range(count)]
    return lax.ppermute(value, axis, pairs)


def after(value, *others):
    return lax.optimization_barrier((value, *others))[0]


def gather(block, kept, axis, count, digits):
    pieces = [kept[None]]
    for stride, radix in reversed(digits):
        held = block[None] if len(pieces) == 1 else jnp.concatenate(pieces, 0)
        for step in range(1, radix):
            pieces.append(send(held, axis, count, stride, radix, -step))
    return pieces


def slots_of(digits):
    slots = [()]
    for _, radix in reversed(digits):
        slots = [(step,) + rest for step in range(radix) for rest in slots]
    return slots


def slot_index(me, digits, steps):
    for (stride, radix), step in zip(digits, steps):
        if step:
            me = moved(me, stride, radix, step)
    return me


def sizes_of(digits):
    sizes, held = [1], 1
    for _, radix in reversed(digits):
        sizes += [held] * (radix - 1)
        held *= radix
    return sizes


def scatter(pieces, axis, count, digits):
    for stride, radix in digits:
        keep = pieces[: len(pieces) - (radix - 1)]
        sent = pieces[len(keep) :]
        got = [send(value, axis, count, stride, radix, step + 1) for step, value in enumerate(sent)]
        at, pieces = 0, []
        for value in keep:
            size = value.shape[0]
            for other in got[::-1]:
                value = value + other[at : at + size]
            at += size
            pieces.append(value)
    return pieces[0][0]


def fetch_kernel(tiles_hbm, vec_hbm, tiles_ref, vec_ref, sems):
    pairs = ((tiles_hbm, tiles_ref), (vec_hbm, vec_ref))
    copies = [pltpu.make_async_copy(a, b, sems.at[i]) for i, (a, b) in enumerate(pairs)]
    for copy in copies:
        copy.start()
    for copy in copies:
        copy.wait()


def fetch(*arrays):
    return pl.pallas_call(
        fetch_kernel,
        out_shape=[jax.ShapeDtypeStruct(a.shape, a.dtype) for a in arrays],
        in_specs=[HBM] * 2,
        out_specs=[VMEM] * 2,
        scratch_shapes=[pltpu.SemaphoreType.DMA((2,))],
        compiler_params=PARAMS,
        cost_estimate=pl.CostEstimate(flops=0, bytes_accessed=8 * 2**20, transcendentals=0),
        name="fetch",
    )(*[pltpu.with_memory_space_constraint(a, pltpu.HBM) for a in arrays])


def products(index_ref, tiles_ref, vec, acc, direct):
    dims = (((1,), (1,)), ((), ())) if direct else (((1,), (0,)), ((), ()))
    slots = tiles_ref.shape[0]
    live = index_ref[2 * slots]
    acc[...] = jnp.zeros_like(acc)
    for t in range(slots):
        row, col = index_ref[t], index_ref[slots + t]
        take, put = (col, row) if direct else (row, col)
        y = lax.dot_general(vec[take], tiles_ref[t], dims, preferred_element_type=jnp.float32)
        acc[put] += jnp.where(t < live, y, 0.0)


def direct_half(index, colset, own, tiles, rows, cols):
    width, size = own[0].shape[1:]
    radix = cols[0][1]
    held = sum(piece.shape[0] for piece in own)
    n_row, n_own = len(colset), len(own)

    def body(index_ref, *refs):
        ins, tiles_ref = refs[: n_row + n_own], refs[n_row + n_own]
        keep_ref, *outs, vec, acc = refs[n_row + n_own + 1 :]
        me_r, me_c = lax.axis_index("row"), lax.axis_index("col")
        where = iter(slots_of(rows))
        for piece in ins[:n_row]:
            for i in range(piece.shape[0]):
                vec[slot_index(me_r, rows, next(where))] = piece[i]
        products(index_ref, tiles_ref, vec, acc, True)
        slots = slots_of(cols)
        for i in range(held):
            keep_ref[i] = acc[slot_index(me_c, cols, slots[i])]
        for step, out in enumerate(outs, 1):
            for i in range(held):
                value = acc[slot_index(me_c, cols, slots[step * held + i])]
                high = value.astype(jnp.bfloat16)
                out[i] = high
                out[held + i] = (value - high.astype(jnp.float32)).astype(jnp.bfloat16)
            at = 2 * held
            for piece in ins[n_row:]:
                for i in range(piece.shape[0]):
                    out[at] = piece[i]
                    at += 1

    return pl.pallas_call(
        body,
        out_shape=[jax.ShapeDtypeStruct((held, width, size), jnp.float32)]
        + [jax.ShapeDtypeStruct((3 * held, width, size), jnp.bfloat16)] * (radix - 1),
        in_specs=[SMEM] + [VMEM] * (n_row + n_own + 1),
        out_specs=[VMEM] * radix,
        scratch_shapes=[
            pltpu.VMEM((math.prod(r for _, r in rows), width, size), jnp.bfloat16),
            pltpu.VMEM((math.prod(r for _, r in cols), width, size), jnp.float32),
        ],
        compiler_params=PARAMS,
        name="direct",
    )(index, *colset, *own, tiles)


def mirror_half(index, own, got, tiles, rows, cols):
    width, size = own[0].shape[1:]
    held = sum(piece.shape[0] for piece in own)
    n_own, n_got = len(own), len(got)
    sizes = sizes_of(rows)

    def body(index_ref, *refs):
        ins, tiles_ref = refs[: n_own + n_got], refs[n_own + n_got]
        *outs, vec, acc = refs[n_own + n_got + 1 :]
        me_r, me_c = lax.axis_index("row"), lax.axis_index("col")
        where = iter(slots_of(cols))
        for piece in ins[:n_own]:
            for i in range(piece.shape[0]):
                vec[slot_index(me_c, cols, next(where))] = piece[i]
        for piece in ins[n_own:]:
            for i in range(held):
                vec[slot_index(me_c, cols, next(where))] = piece[2 * held + i]
        products(index_ref, tiles_ref, vec, acc, False)
        where = iter(slots_of(rows))
        for out in outs:
            for i in range(out.shape[0]):
                out[i] = acc[slot_index(me_r, rows, next(where))]

    return pl.pallas_call(
        body,
        out_shape=[jax.ShapeDtypeStruct((n, width, size), jnp.float32) for n in sizes],
        in_specs=[SMEM] + [VMEM] * (n_own + n_got + 1),
        out_specs=[VMEM] * len(sizes),
        scratch_shapes=[
            pltpu.VMEM((math.prod(r for _, r in cols), width, size), jnp.bfloat16),
            pltpu.VMEM((math.prod(r for _, r in rows), width, size), jnp.float32),
        ],
        compiler_params=PARAMS,
        name="mirror",
    )(index, *own, *got, tiles)


def local(n_rows, n_cols, vectors, tiles, tile_rows, tile_cols, tile_live):
    rows, cols = digits_of(n_rows, 99), digits_of(n_cols, 1)
    inner, outer = cols[0], cols[1:]
    index = jnp.concatenate([tile_rows, tile_cols, tile_live])
    tiles, kept = fetch(tiles, vectors)

    def apply(vec, kept):
        colset = gather(vec, kept, "row", n_rows, rows)
        own = gather(vec, kept, "col", n_cols, outer)
        keep, *packed = direct_half(index, colset, own, tiles, rows, cols)
        got = [send(value, "col", n_cols, *inner, step) for step, value in enumerate(packed, 1)]
        held, at, pieces = keep.shape[0], 0, []
        for size in sizes_of(outer):
            value = keep[at : at + size]
            for other in got[::-1]:
                high, low = other[at : at + size], other[held + at : held + at + size]
                value = value + (high.astype(jnp.float32) + low.astype(jnp.float32))
            at += size
            pieces.append(value)
        if False:
            got[-1] = after(got[-1], pieces[-1])
        mirror = mirror_half(index, own, got, tiles, rows, cols)
        return scatter(pieces, "col", n_cols, outer) + scatter(list(mirror), "row", n_rows, rows)

    first = apply(vectors, kept).astype(jnp.bfloat16)
    second = 2.0 * apply(first, first) - kept.astype(jnp.float32)
    return first, second.astype(jnp.bfloat16)


def solution(mesh):
    both = ("row", "col")
    placed = (P(None, both), P(both, None, None), P(both), P(both), P(both))
    return jax.shard_map(
        functools.partial(local, mesh.shape["row"], mesh.shape["col"]),
        mesh=mesh,
        in_specs=placed,
        out_specs=(P(None, both), P(None, both)),
        check_vma=False,
    )
```

```python
import functools
import math

import jax
import jax.numpy as jnp
from jax import lax
from jax.experimental import pallas as pl
from jax.experimental.pallas import tpu as pltpu
from jax.sharding import PartitionSpec as P

VMEM = pl.BlockSpec(memory_space=pltpu.VMEM)
HBM = pl.BlockSpec(memory_space=pltpu.HBM)
PARAMS = pltpu.CompilerParams(vmem_limit_bytes=16 * 2**20)


def digits_of(count, wide):
    out, stride, rest, prime = [], 1, count, 2
    while rest > 1:
        while rest % prime:
            prime += 1
        radix = 4 if wide > 0 and rest % 4 == 0 else prime
        wide -= 1
        out.append((stride, radix))
        stride, rest = stride * radix, rest // radix
    return out


def moved(index, stride, radix, step):
    if radix & (radix - 1) == 0 and stride & (stride - 1) == 0:
        return index ^ (abs(step) * stride)
    digit = index // stride % radix
    return index + ((digit + step) % radix - digit) * stride


def send(value, axis, count, stride, radix, step):
    pairs = [(i, moved(i, stride, radix, step)) for i in range(count)]
    return lax.ppermute(value, axis, pairs)


def gather(block, kept, axis, count, digits):
    pieces = [kept[None]]
    for stride, radix in reversed(digits):
        held = block[None] if len(pieces) == 1 else jnp.concatenate(pieces, 0)
        for step in range(1, radix):
            pieces.append(send(held, axis, count, stride, radix, -step))
    return pieces


def slots_of(digits):
    slots = [()]
    for _, radix in reversed(digits):
        slots = [(step,) + rest for step in range(radix) for rest in slots]
    return slots


def slot_index(me, digits, steps):
    for (stride, radix), step in zip(digits, steps):
        if step:
            me = moved(me, stride, radix, step)
    return me


def sizes_of(digits):
    sizes, held = [1], 1
    for _, radix in reversed(digits):
        sizes += [held] * (radix - 1)
        held *= radix
    return sizes


def scatter(pieces, axis, count, digits):
    for stride, radix in digits:
        keep = pieces[: len(pieces) - (radix - 1)]
        sent = pieces[len(keep) :]
        got = [send(value, axis, count, stride, radix, step + 1) for step, value in enumerate(sent)]
        at, pieces = 0, []
        for value in keep:
            size = value.shape[0]
            for other in got[::-1]:
                value = value + other[at : at + size]
            at += size
            pieces.append(value)
    return pieces[0][0]


def fetch_kernel(tiles_hbm, vec_hbm, tiles_ref, vec_ref, sems):
    pairs = ((tiles_hbm, tiles_ref), (vec_hbm, vec_ref))
    copies = [pltpu.make_async_copy(a, b, sems.at[i]) for i, (a, b) in enumerate(pairs)]
    for copy in copies:
        copy.start()
    for copy in copies:
        copy.wait()


def fetch(*arrays):
    return pl.pallas_call(
        fetch_kernel,
        out_shape=[jax.ShapeDtypeStruct(a.shape, a.dtype) for a in arrays],
        in_specs=[HBM] * 2,
        out_specs=[VMEM] * 2,
        scratch_shapes=[pltpu.SemaphoreType.DMA((2,))],
        compiler_params=PARAMS,
        cost_estimate=pl.CostEstimate(flops=0, bytes_accessed=8 * 2**20, transcendentals=0),
        name="fetch",
    )(*[pltpu.with_memory_space_constraint(a, pltpu.HBM) for a in arrays])


def products(code_ref, tiles_ref, vec, acc, direct):
    dims = (((1,), (1,)), ((), ())) if direct else (((1,), (0,)), ((), ()))
    acc[...] = jnp.zeros_like(acc)
    for t in range(tiles_ref.shape[0]):
        code = code_ref[t, 0]
        row, col, used = code & 4095, (code >> 12) & 4095, code >> 24
        take, put = (col, row) if direct else (row, col)
        y = lax.dot_general(vec[take], tiles_ref[t], dims, preferred_element_type=jnp.float32)
        acc[put] += jnp.where(used > 0, y, 0.0)


def direct_half(codes, colset, own, tiles, rows, cols):
    width, size = own[0].shape[1:]
    radix = cols[0][1]
    held = sum(piece.shape[0] for piece in own)
    n_row, n_own = len(colset), len(own)

    def body(code_ref, *refs):
        ins, tiles_ref = refs[: n_row + n_own], refs[n_row + n_own]
        keep_ref, *outs, vec, acc = refs[n_row + n_own + 1 :]
        me_r, me_c = lax.axis_index("row"), lax.axis_index("col")
        where = iter(slots_of(rows))
        for piece in ins[:n_row]:
            for i in range(piece.shape[0]):
                vec[slot_index(me_r, rows, next(where))] = piece[i]
        products(code_ref, tiles_ref, vec, acc, True)
        slots = slots_of(cols)
        for i in range(held):
            keep_ref[i] = acc[slot_index(me_c, cols, slots[i])]
        for step, out in enumerate(outs, 1):
            for i in range(held):
                value = acc[slot_index(me_c, cols, slots[step * held + i])]
                high = value.astype(jnp.bfloat16)
                out[i] = high
                out[held + i] = (value - high.astype(jnp.float32)).astype(jnp.bfloat16)
            at = 2 * held
            for piece in ins[n_row:]:
                for i in range(piece.shape[0]):
                    out[at] = piece[i]
                    at += 1

    return pl.pallas_call(
        body,
        out_shape=[jax.ShapeDtypeStruct((held, width, size), jnp.float32)]
        + [jax.ShapeDtypeStruct((3 * held, width, size), jnp.bfloat16)] * (radix - 1),
        in_specs=[VMEM] * (n_row + n_own + 2),
        out_specs=[VMEM] * radix,
        scratch_shapes=[
            pltpu.VMEM((math.prod(r for _, r in rows), width, size), jnp.bfloat16),
            pltpu.VMEM((math.prod(r for _, r in cols), width, size), jnp.float32),
        ],
        compiler_params=PARAMS,
        name="direct",
    )(codes, *colset, *own, tiles)


def mirror_half(codes, own, got, tiles, rows, cols):
    width, size = own[0].shape[1:]
    held = sum(piece.shape[0] for piece in own)
    n_own, n_got = len(own), len(got)
    sizes = sizes_of(rows)

    def body(code_ref, *refs):
        ins, tiles_ref = refs[: n_own + n_got], refs[n_own + n_got]
        *outs, vec, acc = refs[n_own + n_got + 1 :]
        me_r, me_c = lax.axis_index("row"), lax.axis_index("col")
        where = iter(slots_of(cols))
        for piece in ins[:n_own]:
            for i in range(piece.shape[0]):
                vec[slot_index(me_c, cols, next(where))] = piece[i]
        for piece in ins[n_own:]:
            for i in range(held):
                vec[slot_index(me_c, cols, next(where))] = piece[2 * held + i]
        products(code_ref, tiles_ref, vec, acc, False)
        where = iter(slots_of(rows))
        for out in outs:
            for i in range(out.shape[0]):
                out[i] = acc[slot_index(me_r, rows, next(where))]

    return pl.pallas_call(
        body,
        out_shape=[jax.ShapeDtypeStruct((n, width, size), jnp.float32) for n in sizes],
        in_specs=[VMEM] * (n_own + n_got + 2),
        out_specs=[VMEM] * len(sizes),
        scratch_shapes=[
            pltpu.VMEM((math.prod(r for _, r in cols), width, size), jnp.bfloat16),
            pltpu.VMEM((math.prod(r for _, r in rows), width, size), jnp.float32),
        ],
        compiler_params=PARAMS,
        name="mirror",
    )(codes, *own, *got, tiles)


def local(n_rows, n_cols, vectors, tiles, tile_rows, tile_cols, tile_live):
    rows, cols = digits_of(n_rows, 99), digits_of(n_cols, 1)
    inner, outer = cols[0], cols[1:]
    used = (jnp.arange(tile_rows.shape[0], dtype=jnp.int32) < tile_live[0]).astype(jnp.int32)
    codes = jnp.broadcast_to((tile_rows + tile_cols * 4096 + used * 4096**2)[:, None], (tile_rows.shape[0], 128))
    tiles, kept = fetch(tiles, vectors)

    def apply(vec, kept):
        colset = gather(vec, kept, "row", n_rows, rows)
        own = gather(vec, kept, "col", n_cols, outer)
        keep, *packed = direct_half(codes, colset, own, tiles, rows, cols)
        got = [send(value, "col", n_cols, *inner, step) for step, value in enumerate(packed, 1)]
        held, at, pieces = keep.shape[0], 0, []
        for size in sizes_of(outer):
            value = keep[at : at + size]
            for other in got[::-1]:
                high, low = other[at : at + size], other[held + at : held + at + size]
                value = value + (high.astype(jnp.float32) + low.astype(jnp.float32))
            at += size
            pieces.append(value)
        mirror = mirror_half(codes, own, got, tiles, rows, cols)
        return scatter(pieces, "col", n_cols, outer) + scatter(list(mirror), "row", n_rows, rows)

    first = apply(vectors, kept).astype(jnp.bfloat16)
    second = 2.0 * apply(first, first) - kept.astype(jnp.float32)
    return first, second.astype(jnp.bfloat16)


def solution(mesh):
    both = ("row", "col")
    placed = (P(None, both), P(both, None, None), P(both), P(both), P(both))
    return jax.shard_map(
        functools.partial(local, mesh.shape["row"], mesh.shape["col"]),
        mesh=mesh,
        in_specs=placed,
        out_specs=(P(None, both), P(None, both)),
        check_vma=False,
    )
```

```python
import functools
import math

import jax
import jax.numpy as jnp
from jax import lax
from jax.experimental import pallas as pl
from jax.experimental.pallas import tpu as pltpu
from jax.sharding import PartitionSpec as P

VMEM = pl.BlockSpec(memory_space=pltpu.VMEM)
HBM = pl.BlockSpec(memory_space=pltpu.HBM)
PARAMS = pltpu.CompilerParams(vmem_limit_bytes=16 * 2**20)


def digits_of(count, wide):
    out, stride, rest, prime = [], 1, count, 2
    while rest > 1:
        while rest % prime:
            prime += 1
        radix = 4 if wide > 0 and rest % 4 == 0 else prime
        wide -= 1
        out.append((stride, radix))
        stride, rest = stride * radix, rest // radix
    return out


def moved(index, stride, radix, step):
    if radix & (radix - 1) == 0 and stride & (stride - 1) == 0:
        return index ^ (abs(step) * stride)
    digit = index // stride % radix
    return index + ((digit + step) % radix - digit) * stride


def send(value, axis, count, stride, radix, step):
    pairs = [(i, moved(i, stride, radix, step)) for i in range(count)]
    return lax.ppermute(value, axis, pairs)


def gather(block, kept, axis, count, digits):
    pieces = [kept[None]]
    for stride, radix in reversed(digits):
        held = block[None] if len(pieces) == 1 else jnp.concatenate(pieces, 0)
        for step in range(1, radix):
            pieces.append(send(held, axis, count, stride, radix, -step))
    return pieces


def slots_of(digits):
    slots = [()]
    for _, radix in reversed(digits):
        slots = [(step,) + rest for step in range(radix) for rest in slots]
    return slots


def slot_index(me, digits, steps):
    for (stride, radix), step in zip(digits, steps):
        if step:
            me = moved(me, stride, radix, step)
    return me


def sizes_of(digits):
    sizes, held = [1], 1
    for _, radix in reversed(digits):
        sizes += [held] * (radix - 1)
        held *= radix
    return sizes


def scatter(pieces, axis, count, digits):
    for stride, radix in digits:
        keep = pieces[: len(pieces) - (radix - 1)]
        sent = pieces[len(keep) :]
        got = [send(value, axis, count, stride, radix, step + 1) for step, value in enumerate(sent)]
        at, pieces = 0, []
        for value in keep:
            size = value.shape[0]
            for other in got[::-1]:
                value = value + other[at : at + size]
            at += size
            pieces.append(value)
    return pieces[0][0]


def fetch_kernel(tiles_hbm, vec_hbm, rows_hbm, cols_hbm, live_ref, tiles_ref, vec_ref, codes_ref, rows_ref, cols_ref, sems):
    pairs = ((tiles_hbm, tiles_ref), (vec_hbm, vec_ref), (rows_hbm, rows_ref), (cols_hbm, cols_ref))
    copies = [pltpu.make_async_copy(a, b, sems.at[i]) for i, (a, b) in enumerate(pairs)]
    for copy in copies:
        copy.start()
    for copy in copies[2:]:
        copy.wait()
    slots = rows_ref.shape[0]
    slot = lax.broadcasted_iota(jnp.int32, (slots, slots), 0)
    lane = lax.broadcasted_iota(jnp.int32, (slots, slots), 1)
    code = rows_ref[...] + cols_ref[...] * 4096
    code = jnp.sum(jnp.where(slot == lane, code[None, :], 0), 1, keepdims=True)
    used = lax.broadcasted_iota(jnp.int32, (slots, 128), 0) < live_ref[0]
    codes_ref[...] = code + jnp.where(used, 4096**2, 0)
    for copy in copies[:2]:
        copy.wait()


def fetch(tiles, vectors, tile_rows, tile_cols, tile_live):
    slots = tile_rows.shape[0]
    pinned = [pltpu.with_memory_space_constraint(a, pltpu.HBM) for a in (tiles, vectors, tile_rows, tile_cols)]
    return pl.pallas_call(
        fetch_kernel,
        out_shape=[
            jax.ShapeDtypeStruct(tiles.shape, tiles.dtype),
            jax.ShapeDtypeStruct(vectors.shape, vectors.dtype),
            jax.ShapeDtypeStruct((slots, 128), jnp.int32),
        ],
        in_specs=[HBM] * 4 + [pl.BlockSpec(memory_space=pltpu.SMEM)],
        out_specs=[VMEM] * 3,
        scratch_shapes=[
            pltpu.VMEM((slots,), jnp.int32),
            pltpu.VMEM((slots,), jnp.int32),
            pltpu.SemaphoreType.DMA((4,)),
        ],
        compiler_params=PARAMS,
        cost_estimate=pl.CostEstimate(flops=0, bytes_accessed=8 * 2**20, transcendentals=0),
        name="fetch",
    )(*pinned, tile_live)


def turn_kernel(tiles_ref, out_ref):
    for t in range(tiles_ref.shape[0]):
        out_ref[t] = tiles_ref[t].T


def turn(tiles):
    return pl.pallas_call(
        turn_kernel,
        out_shape=jax.ShapeDtypeStruct(tiles.shape, tiles.dtype),
        in_specs=[VMEM],
        out_specs=VMEM,
        compiler_params=PARAMS,
        name="turn",
    )(tiles)


def products(code_ref, tiles_ref, vec, acc, direct, turned=False):
    dims = (((1,), (1,)), ((), ())) if direct and not turned else (((1,), (0,)), ((), ()))
    acc[...] = jnp.zeros_like(acc)
    for t in range(tiles_ref.shape[0]):
        code = code_ref[t, 0]
        row, col, used = code & 4095, (code >> 12) & 4095, code >> 24
        take, put = (col, row) if direct else (row, col)
        y = lax.dot_general(vec[take], tiles_ref[t], dims, preferred_element_type=jnp.float32)
        acc[put] += jnp.where(used > 0, y, 0.0)


def direct_half(codes, colset, own, tiles, rows, cols, turned=False):
    width, size = own[0].shape[1:]
    radix = cols[0][1]
    held = sum(piece.shape[0] for piece in own)
    n_row, n_own = len(colset), len(own)

    def body(code_ref, *refs):
        ins, tiles_ref = refs[: n_row + n_own], refs[n_row + n_own]
        keep_ref, *outs, vec, acc = refs[n_row + n_own + 1 :]
        me_r, me_c = lax.axis_index("row"), lax.axis_index("col")
        where = iter(slots_of(rows))
        for piece in ins[:n_row]:
            for i in range(piece.shape[0]):
                vec[slot_index(me_r, rows, next(where))] = piece[i]
        products(code_ref, tiles_ref, vec, acc, True, turned)
        slots = slots_of(cols)
        for i in range(held):
            keep_ref[i] = acc[slot_index(me_c, cols, slots[i])]
        for step, out in enumerate(outs, 1):
            for i in range(held):
                value = acc[slot_index(me_c, cols, slots[step * held + i])]
                high = value.astype(jnp.bfloat16)
                out[i] = high
                out[held + i] = (value - high.astype(jnp.float32)).astype(jnp.bfloat16)
            at = 2 * held
            for piece in ins[n_row:]:
                for i in range(piece.shape[0]):
                    out[at] = piece[i]
                    at += 1

    return pl.pallas_call(
        body,
        out_shape=[jax.ShapeDtypeStruct((held, width, size), jnp.float32)]
        + [jax.ShapeDtypeStruct((3 * held, width, size), jnp.bfloat16)] * (radix - 1),
        in_specs=[VMEM] * (n_row + n_own + 2),
        out_specs=[VMEM] * radix,
        scratch_shapes=[
            pltpu.VMEM((math.prod(r for _, r in rows), width, size), jnp.bfloat16),
            pltpu.VMEM((math.prod(r for _, r in cols), width, size), jnp.float32),
        ],
        compiler_params=PARAMS,
        name="direct",
    )(codes, *colset, *own, tiles)


def mirror_half(codes, own, got, tiles, rows, cols):
    width, size = own[0].shape[1:]
    held = sum(piece.shape[0] for piece in own)
    n_own, n_got = len(own), len(got)
    sizes = sizes_of(rows)

    def body(code_ref, *refs):
        ins, tiles_ref = refs[: n_own + n_got], refs[n_own + n_got]
        *outs, vec, acc = refs[n_own + n_got + 1 :]
        me_r, me_c = lax.axis_index("row"), lax.axis_index("col")
        where = iter(slots_of(cols))
        for piece in ins[:n_own]:
            for i in range(piece.shape[0]):
                vec[slot_index(me_c, cols, next(where))] = piece[i]
        for piece in ins[n_own:]:
            for i in range(held):
                vec[slot_index(me_c, cols, next(where))] = piece[2 * held + i]
        products(code_ref, tiles_ref, vec, acc, False)
        where = iter(slots_of(rows))
        for out in outs:
            for i in range(out.shape[0]):
                out[i] = acc[slot_index(me_r, rows, next(where))]

    return pl.pallas_call(
        body,
        out_shape=[jax.ShapeDtypeStruct((n, width, size), jnp.float32) for n in sizes],
        in_specs=[VMEM] * (n_own + n_got + 2),
        out_specs=[VMEM] * len(sizes),
        scratch_shapes=[
            pltpu.VMEM((math.prod(r for _, r in cols), width, size), jnp.bfloat16),
            pltpu.VMEM((math.prod(r for _, r in rows), width, size), jnp.float32),
        ],
        compiler_params=PARAMS,
        name="mirror",
    )(codes, *own, *got, tiles)


def local(n_rows, n_cols, vectors, tiles, tile_rows, tile_cols, tile_live):
    rows, cols = digits_of(n_rows, 99), digits_of(n_cols, 1)
    inner, outer = cols[0], cols[1:]
    tiles, kept, codes = fetch(tiles, vectors, tile_rows, tile_cols, tile_live)

    turned = turn(tiles)

    def apply(vec, kept, again):
        colset = gather(vec, kept, "row", n_rows, rows)
        own = gather(vec, kept, "col", n_cols, outer)
        keep, *packed = direct_half(codes, colset, own, turned if again else tiles, rows, cols, again)
        got = [send(value, "col", n_cols, *inner, step) for step, value in enumerate(packed, 1)]
        held, at, pieces = keep.shape[0], 0, []
        for size in sizes_of(outer):
            value = keep[at : at + size]
            for other in got[::-1]:
                high, low = other[at : at + size], other[held + at : held + at + size]
                value = value + (high.astype(jnp.float32) + low.astype(jnp.float32))
            at += size
            pieces.append(value)
        mirror = mirror_half(codes, own, got, tiles, rows, cols)
        return scatter(pieces, "col", n_cols, outer) + scatter(list(mirror), "row", n_rows, rows)

    first = apply(vectors, kept, False).astype(jnp.bfloat16)
    second = 2.0 * apply(first, first, True) - kept.astype(jnp.float32)
    return first, second.astype(jnp.bfloat16)


def solution(mesh):
    both = ("row", "col")
    placed = (P(None, both), P(both, None, None), P(both), P(both), P(both))
    return jax.shard_map(
        functools.partial(local, mesh.shape["row"], mesh.shape["col"]),
        mesh=mesh,
        in_specs=placed,
        out_specs=(P(None, both), P(None, both)),
        check_vma=False,
    )
```

```python
import functools
import math

import jax
import jax.numpy as jnp
from jax import lax
from jax.experimental import pallas as pl
from jax.experimental.pallas import tpu as pltpu
from jax.sharding import PartitionSpec as P

VMEM = pl.BlockSpec(memory_space=pltpu.VMEM)
HBM = pl.BlockSpec(memory_space=pltpu.HBM)
PARAMS = pltpu.CompilerParams(vmem_limit_bytes=16 * 2**20)


def digits_of(count, wide):
    out, stride, rest, prime = [], 1, count, 2
    while rest > 1:
        while rest % prime:
            prime += 1
        radix = 4 if wide > 0 and rest % 4 == 0 else prime
        wide -= 1
        out.append((stride, radix))
        stride, rest = stride * radix, rest // radix
    return out


def moved(index, stride, radix, step):
    if radix & (radix - 1) == 0 and stride & (stride - 1) == 0:
        return index ^ (abs(step) * stride)
    digit = index // stride % radix
    return index + ((digit + step) % radix - digit) * stride


def send(value, axis, count, stride, radix, step):
    pairs = [(i, moved(i, stride, radix, step)) for i in range(count)]
    return lax.ppermute(value, axis, pairs)


def gather(block, kept, axis, count, digits):
    pieces = [kept[None]]
    for stride, radix in reversed(digits):
        held = block[None] if len(pieces) == 1 else jnp.concatenate(pieces, 0)
        for step in range(1, radix):
            pieces.append(send(held, axis, count, stride, radix, -step))
    return pieces


def slots_of(digits):
    slots = [()]
    for _, radix in reversed(digits):
        slots = [(step,) + rest for step in range(radix) for rest in slots]
    return slots


def twisted(step, odd):
    return (0, 1 + odd, 2 - odd, 3)[step]


def slot_index(me, digits, steps, odd=None):
    for turn, ((stride, radix), step) in enumerate(zip(digits, steps)):
        if step and turn == 0 and radix == 4 and odd is not None:
            me = me ^ (twisted(step, odd) * stride)
        elif step:
            me = moved(me, stride, radix, step)
    return me


def send_twisted(value, n_rows, n_cols, stride, radix, step):
    if radix != 4:
        return send(value, "col", n_cols, stride, radix, step)
    pairs = [
        (row * n_cols + col, row * n_cols + (col ^ (twisted(step, row & 1) * stride)))
        for row in range(n_rows)
        for col in range(n_cols)
    ]
    return lax.ppermute(value, ("row", "col"), pairs)


def sizes_of(digits):
    sizes, held = [1], 1
    for _, radix in reversed(digits):
        sizes += [held] * (radix - 1)
        held *= radix
    return sizes


def scatter(pieces, axis, count, digits):
    for stride, radix in digits:
        keep = pieces[: len(pieces) - (radix - 1)]
        sent = pieces[len(keep) :]
        got = [send(value, axis, count, stride, radix, step + 1) for step, value in enumerate(sent)]
        at, pieces = 0, []
        for value in keep:
            size = value.shape[0]
            for other in got[::-1]:
                value = value + other[at : at + size]
            at += size
            pieces.append(value)
    return pieces[0][0]


def fetch_kernel(tiles_hbm, vec_hbm, rows_hbm, cols_hbm, live_ref, tiles_ref, vec_ref, codes_ref, rows_ref, cols_ref, sems):
    pairs = ((tiles_hbm, tiles_ref), (vec_hbm, vec_ref), (rows_hbm, rows_ref), (cols_hbm, cols_ref))
    copies = [pltpu.make_async_copy(a, b, sems.at[i]) for i, (a, b) in enumerate(pairs)]
    for copy in copies:
        copy.start()
    for copy in copies[2:]:
        copy.wait()
    slots = rows_ref.shape[0]
    slot = lax.broadcasted_iota(jnp.int32, (slots, slots), 0)
    lane = lax.broadcasted_iota(jnp.int32, (slots, slots), 1)
    code = rows_ref[...] + cols_ref[...] * 4096
    code = jnp.sum(jnp.where(slot == lane, code[None, :], 0), 1, keepdims=True)
    used = lax.broadcasted_iota(jnp.int32, (slots, 128), 0) < live_ref[0]
    codes_ref[...] = code + jnp.where(used, 4096**2, 0)
    for copy in copies[:2]:
        copy.wait()


def fetch(tiles, vectors, tile_rows, tile_cols, tile_live):
    slots = tile_rows.shape[0]
    pinned = [pltpu.with_memory_space_constraint(a, pltpu.HBM) for a in (tiles, vectors, tile_rows, tile_cols)]
    return pl.pallas_call(
        fetch_kernel,
        out_shape=[
            jax.ShapeDtypeStruct(tiles.shape, tiles.dtype),
            jax.ShapeDtypeStruct(vectors.shape, vectors.dtype),
            jax.ShapeDtypeStruct((slots, 128), jnp.int32),
        ],
        in_specs=[HBM] * 4 + [pl.BlockSpec(memory_space=pltpu.SMEM)],
        out_specs=[VMEM] * 3,
        scratch_shapes=[
            pltpu.VMEM((slots,), jnp.int32),
            pltpu.VMEM((slots,), jnp.int32),
            pltpu.SemaphoreType.DMA((4,)),
        ],
        compiler_params=PARAMS,
        cost_estimate=pl.CostEstimate(flops=0, bytes_accessed=8 * 2**20, transcendentals=0),
        name="fetch",
    )(*pinned, tile_live)


def turn_kernel(tiles_ref, out_ref):
    for t in range(tiles_ref.shape[0]):
        out_ref[t] = tiles_ref[t].T


def turn(tiles):
    return pl.pallas_call(
        turn_kernel,
        out_shape=jax.ShapeDtypeStruct(tiles.shape, tiles.dtype),
        in_specs=[VMEM],
        out_specs=VMEM,
        compiler_params=PARAMS,
        name="turn",
    )(tiles)


def products(code_ref, tiles_ref, vec, acc, direct, turned=False):
    dims = (((1,), (1,)), ((), ())) if direct and not turned else (((1,), (0,)), ((), ()))
    acc[...] = jnp.zeros_like(acc)
    for t in range(tiles_ref.shape[0]):
        code = code_ref[t, 0]
        row, col, used = code & 4095, (code >> 12) & 4095, code >> 24
        take, put = (col, row) if direct else (row, col)
        y = lax.dot_general(vec[take], tiles_ref[t], dims, preferred_element_type=jnp.float32)
        acc[put] += jnp.where(used > 0, y, 0.0)


def direct_half(codes, colset, own, tiles, rows, cols, turned=False):
    width, size = own[0].shape[1:]
    radix = cols[0][1]
    held = sum(piece.shape[0] for piece in own)
    n_row, n_own = len(colset), len(own)

    def body(code_ref, *refs):
        ins, tiles_ref = refs[: n_row + n_own], refs[n_row + n_own]
        keep_ref, *outs, vec, acc = refs[n_row + n_own + 1 :]
        me_r, me_c = lax.axis_index("row"), lax.axis_index("col")
        where = iter(slots_of(rows))
        for piece in ins[:n_row]:
            for i in range(piece.shape[0]):
                vec[slot_index(me_r, rows, next(where))] = piece[i]
        products(code_ref, tiles_ref, vec, acc, True, turned)
        slots = slots_of(cols)
        for i in range(held):
            keep_ref[i] = acc[slot_index(me_c, cols, slots[i], me_r & 1)]
        for step, out in enumerate(outs, 1):
            for i in range(held):
                value = acc[slot_index(me_c, cols, slots[step * held + i], me_r & 1)]
                high = value.astype(jnp.bfloat16)
                out[i] = high
                out[held + i] = (value - high.astype(jnp.float32)).astype(jnp.bfloat16)
            at = 2 * held
            for piece in ins[n_row:]:
                for i in range(piece.shape[0]):
                    out[at] = piece[i]
                    at += 1

    return pl.pallas_call(
        body,
        out_shape=[jax.ShapeDtypeStruct((held, width, size), jnp.float32)]
        + [jax.ShapeDtypeStruct((3 * held, width, size), jnp.bfloat16)] * (radix - 1),
        in_specs=[VMEM] * (n_row + n_own + 2),
        out_specs=[VMEM] * radix,
        scratch_shapes=[
            pltpu.VMEM((math.prod(r for _, r in rows), width, size), jnp.bfloat16),
            pltpu.VMEM((math.prod(r for _, r in cols), width, size), jnp.float32),
        ],
        compiler_params=PARAMS,
        name="direct",
    )(codes, *colset, *own, tiles)


def mirror_half(codes, own, got, tiles, rows, cols):
    width, size = own[0].shape[1:]
    held = sum(piece.shape[0] for piece in own)
    n_own, n_got = len(own), len(got)
    sizes = sizes_of(rows)

    def body(code_ref, *refs):
        ins, tiles_ref = refs[: n_own + n_got], refs[n_own + n_got]
        *outs, vec, acc = refs[n_own + n_got + 1 :]
        me_r, me_c = lax.axis_index("row"), lax.axis_index("col")
        where = iter(slots_of(cols))
        for piece in ins[:n_own]:
            for i in range(piece.shape[0]):
                vec[slot_index(me_c, cols, next(where), me_r & 1)] = piece[i]
        for piece in ins[n_own:]:
            for i in range(held):
                vec[slot_index(me_c, cols, next(where), me_r & 1)] = piece[2 * held + i]
        products(code_ref, tiles_ref, vec, acc, False)
        where = iter(slots_of(rows))
        for out in outs:
            for i in range(out.shape[0]):
                out[i] = acc[slot_index(me_r, rows, next(where))]

    return pl.pallas_call(
        body,
        out_shape=[jax.ShapeDtypeStruct((n, width, size), jnp.float32) for n in sizes],
        in_specs=[VMEM] * (n_own + n_got + 2),
        out_specs=[VMEM] * len(sizes),
        scratch_shapes=[
            pltpu.VMEM((math.prod(r for _, r in cols), width, size), jnp.bfloat16),
            pltpu.VMEM((math.prod(r for _, r in rows), width, size), jnp.float32),
        ],
        compiler_params=PARAMS,
        name="mirror",
    )(codes, *own, *got, tiles)


def local(n_rows, n_cols, vectors, tiles, tile_rows, tile_cols, tile_live):
    rows, cols = digits_of(n_rows, 99), digits_of(n_cols, 1)
    inner, outer = cols[0], cols[1:]
    tiles, kept, codes = fetch(tiles, vectors, tile_rows, tile_cols, tile_live)

    turned = turn(tiles)

    def apply(vec, kept, again):
        colset = gather(vec, kept, "row", n_rows, rows)
        own = gather(vec, kept, "col", n_cols, outer)
        keep, *packed = direct_half(codes, colset, own, turned if again else tiles, rows, cols, again)
        got = [send_twisted(value, n_rows, n_cols, *inner, step) for step, value in enumerate(packed, 1)]
        held, at, pieces = keep.shape[0], 0, []
        for size in sizes_of(outer):
            value = keep[at : at + size]
            for other in got[::-1]:
                high, low = other[at : at + size], other[held + at : held + at + size]
                value = value + (high.astype(jnp.float32) + low.astype(jnp.float32))
            at += size
            pieces.append(value)
        mirror = mirror_half(codes, own, got, tiles, rows, cols)
        return scatter(pieces, "col", n_cols, outer) + scatter(list(mirror), "row", n_rows, rows)

    first = apply(vectors, kept, False).astype(jnp.bfloat16)
    second = 2.0 * apply(first, first, True) - kept.astype(jnp.float32)
    return first, second.astype(jnp.bfloat16)


def solution(mesh):
    both = ("row", "col")
    placed = (P(None, both), P(both, None, None), P(both), P(both), P(both))
    return jax.shard_map(
        functools.partial(local, mesh.shape["row"], mesh.shape["col"]),
        mesh=mesh,
        in_specs=placed,
        out_specs=(P(None, both), P(None, both)),
        check_vma=False,
    )
```
